32 devices in a mesh: row: 4 (over z), col: 4 (over y, core), ens: 2 (over x).
Axes of the slice: x: 2, y: 2, z: 4, core: 2. Of those that a mesh axis runs over, the one named last changes fastest.
Arguments:
- fourier: bfloat16 [720, 64, 1024], P('row', 'col', 'ens'), parts along dimension 2, may hold values from -6 to 6
- legendre: bfloat16 [720, 11264], P('row', 'col'), may hold values from -0.21875 to 0.21875
- lag_weights: float32 [3, 22528], P(None, 'col'), may hold values from -0.9 to 0.9
- pair_order: int32 [16], P('col'), may hold values from 0 to 15, each once
Outputs:
- zero_lag: bfloat16 [22528, 22528], P(('ens', 'row'), 'col'), parts along dimension 0
- one_lag: bfloat16 [22528, 22528], P(('ens', 'row'), 'col'), parts along dimension 0
The draws below stay inside these ranges and needn't reach their ends.
There are 2 independent parts, one for each index of `ens`. The reference program is written for one: setup_inputs(seed, part) draws one part's arguments, and reference() takes and returns one part's arrays. A program takes and returns all parts, laid end to end along the dimension named above; an argument that names none is the same for every part. Nothing has to cross between parts.
Inputs may be any that keep to these rules, and one draw needn't show every extreme that they name: `pair_order`: a permutation of 0 to 15.
All inputs are finite; a program needn't handle non-finite values.
Results may differ from the reference program's by a relative error of at most 0.0057.
Values may be sent and summed in bfloat16 or wider, within the bound.
No kernel may reach another device: no remote copies, remote signals or barrier semaphores. Data moves between devices by JAX's collectives and lax.ppermute only.
A program may use at most 128 MiB of HBM per device.

```python
import jax
import jax.numpy as jnp

DEG = 703
PAIRS = 16
CYCLES = 720
HALF = 11264
COV = 22528
COVR = 11264
FREQ = 64
DAYS = 512


def block_scale(stream_key, extent, shards, low, largest):
    def one(position, shards_of):
        steps = jax.random.uniform(jax.random.fold_in(jax.random.fold_in(stream_key, 6), position), (shards_of,), jnp.float32, low / len(shards), largest / len(shards))
        return jnp.repeat(jnp.exp(steps), extent[position] // shards_of).reshape((-1,) + (1,) * (len(extent) - position - 1))

    gain = one(*shards[0])
    for cut in shards[1:]:
        gain = gain * one(*cut)
    return gain


def scatter_about(stream_key, extent, deviation, limit, shards=(), held_as=jnp.bfloat16):
    values = jax.random.normal(stream_key, extent, jnp.float32) * deviation
    if len(shards) > 0:
        values = block_scale(stream_key, extent, shards, -0.22, 0.18) * values
    return jnp.clip(values, min=-limit, max=limit).astype(held_as)


def setup_inputs(seed: int = 0, part: int = 0) -> dict:
    splits = jax.random.split(jax.random.key(seed), 5)
    own_keys = jax.random.split(jax.random.fold_in(splits[4], part), 5)
    fourier = scatter_about(own_keys[0], (CYCLES, FREQ, DAYS), 1.0, 6.0, ((0, 4), (1, 4)))
    legendre = scatter_about(splits[1], (CYCLES, HALF), CYCLES ** -0.5, 0.21875, ((0, 4), (1, 4)))
    lag_weights = jnp.clip(jax.random.uniform(splits[2], (3, COV), jnp.float32, -0.9, 0.9) * block_scale(splits[2], (3, COV), ((1, 4),), -0.4, 0.0), -0.9, 0.9)
    pair_order = jax.random.permutation(splits[3], PAIRS).astype(jnp.int32)
    return dict(fourier=fourier, legendre=legendre, lag_weights=lag_weights, pair_order=pair_order)


def analyse(fourier, legendre, pair_order):
    degree_cols = DEG + 1
    boundary = DEG - pair_order
    column = jnp.arange(degree_cols, dtype=jnp.int32)
    leading = column[None, :] < boundary[:, None]
    selector = jnp.stack([leading, jnp.logical_not(leading)], axis=1).astype(jnp.float32)
    masked = legendre.astype(jnp.float32).reshape(CYCLES, PAIRS, 1, degree_cols) * selector[None]
    spectra = fourier.astype(jnp.float32).reshape(CYCLES, PAIRS, 2, 2, DAYS)
    spectral = jnp.einsum("rpowd,rpoj->dpwj", spectra, masked)
    return spectral.reshape(DAYS, COV)


def reference(fourier, legendre, lag_weights, pair_order):
    spectral = analyse(fourier, legendre, pair_order)
    filtered = spectral[3:] - lag_weights[0] * spectral[2:-1] - lag_weights[1] * spectral[1:-2] - lag_weights[2] * spectral[:-3]
    residual = jnp.concatenate([jnp.zeros((3, COV), jnp.float32), filtered], axis=0).astype(jnp.bfloat16)
    slab_rows = residual[:, :COVR]
    zero_lag = jnp.dot(slab_rows.T, residual, preferred_element_type=jnp.float32) * (1.0 / (DAYS - 3))
    one_lag = jnp.dot(slab_rows[1:].T, residual[:-1], preferred_element_type=jnp.float32) * (1.0 / (DAYS - 4))
    return zero_lag.astype(jnp.bfloat16), one_lag.astype(jnp.bfloat16)
```

```python
import functools

import jax
import jax.numpy as jnp
from jax import lax
from jax.experimental import pallas as pl
from jax.experimental.pallas import tpu as pltpu
from jax.sharding import PartitionSpec as P


def after(x, *deps):
    return lax.optimization_barrier((x,) + deps)[0]


class Line:
    def __init__(self, block, rows, route=None):
        self.rows = rows
        self.route = route
        self.left, self.right = [block], [block]

    def hop(self, *deps):
        d = len(self.left)
        n = self.rows
        up, down = self.left[-1], self.right[-1]
        if deps:
            up, down = after(up, *deps), after(down, *deps)
        if self.route is None:
            axis = "row"
            ups = [(i, i + 1) for i in range(d - 1, n - 1)]
            downs = [(i, i - 1) for i in range(1, n - d + 1)]
        else:
            axis = ("row", "col")
            cols = lax.axis_size("col")
            ups, downs = [], []
            for target, col in self.route:
                for i in range(d - 1, target):
                    ups.append((i * cols + col, (i + 1) * cols + col))
                for i in range(target + 1, n - d + 1):
                    downs.append((i * cols + col, (i - 1) * cols + col))
        self.left.append(lax.ppermute(up, axis, ups) if ups else jnp.zeros_like(up))
        self.right.append(lax.ppermute(down, axis, downs) if downs else jnp.zeros_like(down))
        return self.left[-1], self.right[-1]

    def slots(self):
        z = lax.axis_index("row")
        out = [self.left[0]]
        for d in range(1, self.rows):
            out.append(jnp.where(z >= d, self.left[d], self.right[self.rows - d]))
        return out


def cov_kernel(place, lhs, lhs_next, col, *refs):
    zero, one = refs[-2:]
    total = col.shape[0]
    zero[...] = (
        jnp.dot(lhs[...], col[...], preferred_element_type=jnp.float32) * (1.0 / (total - 3))
    ).astype(zero.dtype)
    one[...] = (
        jnp.dot(lhs_next[...], col[...], preferred_element_type=jnp.float32) * (1.0 / (total - 4))
    ).astype(one.dtype)


def covariance(place, lhs, lhs_next, col, outs, width):
    rows, days = lhs.shape
    chunk = col.shape[1]
    tile = rows // 8
    in_specs = [
        pl.BlockSpec((tile, days), lambda i, place: (i, 0)),
        pl.BlockSpec((tile, days), lambda i, place: (i, 0)),
        pl.BlockSpec((days, chunk), lambda i, place: (0, 0)),
    ]
    operands = [lhs, lhs_next, col]
    aliases = {}
    if outs is not None:
        in_specs += [pl.BlockSpec(memory_space=pl.ANY)] * 2
        aliases = {4: 0, 5: 1}
        operands += list(outs)
    shape = jax.ShapeDtypeStruct((rows, width), jnp.bfloat16)
    return pl.pallas_call(
        cov_kernel,
        grid_spec=pltpu.PrefetchScalarGridSpec(
            num_scalar_prefetch=1,
            grid=(rows // tile,),
            in_specs=in_specs,
            out_specs=[pl.BlockSpec((tile, chunk), lambda i, place: (i, place[0]))] * 2,
        ),
        out_shape=[shape, shape],
        input_output_aliases=aliases,
        cost_estimate=pl.CostEstimate(
            flops=4 * rows * days * chunk, bytes_accessed=4 * rows * chunk, transcendentals=0
        ),
        name="covariance",
    )(place, *operands)


def body(fourier, legendre, lag_weights, pair_order):
    cycles, _, days = fourier.shape
    pairs = pair_order.shape[0]
    degree_cols = legendre.shape[1] // pairs
    part_cols = lag_weights.shape[1]
    rows, cols, members = (lax.axis_size(a) for a in ("row", "col", "ens"))
    z, c, e = (lax.axis_index(a) for a in ("row", "col", "ens"))
    all_pairs = pairs * cols
    lead = degree_cols - all_pairs
    row_pairs = all_pairs // 2 // rows
    row_cols = row_pairs * 2 * degree_cols

    def first_of(col):
        return (pairs // 2) * (col % 2)

    owner = [r * row_pairs // pairs for r in range(rows)]
    local = [r * row_pairs % pairs for r in range(rows)]
    early = [(local[r] - first_of(owner[r])) % pairs == 0 for r in range(rows)]
    late = [(r, owner[r]) for r in range(rows) if not early[r]]
    assert len(set(col for _, col in late)) == len(late)

    order = [lax.rem(k + first_of(c), pairs) for k in range(pairs)]

    spectra = fourier.reshape(cycles, pairs, 2, 2, days)
    zeroth = spectra[:, :, 0].transpose(1, 0, 2, 3).reshape(pairs, cycles, 2 * days)

    share = members == 2 and pairs % 2 == 0
    half = pairs // 2 * degree_cols
    mine = lax.dynamic_slice(legendre, (0, e * half), (cycles, half)) if share else legendre
    leg = Line(mine, rows)
    swapped_left, swapped_right = [None], [None]

    def swap(block, d, up):
        pairs_of = []
        for r in range(rows):
            if (r >= d) if up else (r + d < rows):
                pairs_of += [(2 * r, 2 * r + 1), (2 * r + 1, 2 * r)]
        return lax.ppermute(block, ("row", "ens"), pairs_of)

    history = []

    def run(line, extra=()):
        deps = history[-2] if len(history) >= 2 else ()
        history.append(line.hop(*deps, *extra))
        return history[-1]

    chunks = [Line(lax.dynamic_index_in_dim(zeroth, order[k], 0, False), rows) for k in range(pairs)]
    row_first = jnp.asarray(local, jnp.int32)[z]
    lines = []
    if late:
        row_own = lax.dynamic_slice(zeroth, (row_first, 0, 0), (row_pairs, cycles, 2 * days))
        wanted = jnp.zeros((), jnp.int32)
        for r, col in late:
            wanted = jnp.where(c == col, local[r], wanted)
        early_rows = Line(
            lax.dynamic_slice(zeroth, (wanted, 0, 0), (row_pairs, cycles, 2 * days)), rows, late
        )

    def leg_hop():
        run(leg)
        d = len(leg.left) - 1
        if share:
            swapped_left.append(swap(leg.left[d], d, True))
            swapped_right.append(swap(leg.right[d], d, False))

    steps = []
    for d in range(1, rows):
        leg_hop()
        if d < rows - 1 and late:
            run(early_rows)
        elif d == rows - 1:
            run(chunks[0])
    if late:
        while len(early_rows.left) < rows:
            early_rows.left.append(jnp.zeros_like(early_rows.left[0]))
            early_rows.right.append(jnp.zeros_like(early_rows.right[0]))

    boundary = degree_cols - 1 - pair_order
    last = legendre.reshape(cycles, pairs, degree_cols)[:, :, lead:]
    tail_own = jnp.einsum(
        "cpwd,cpj->dpwj", spectra[:, :, 1], last, preferred_element_type=jnp.float32
    ).reshape(days, pairs * 2 * all_pairs)
    up = down = None
    tail = tail_own
    for d in range(1, rows):
        send = tail_own if up is None else tail_own + up
        up = lax.ppermute(send, "row", [(d - 1, d)])
        send = tail_own if down is None else tail_own + down
        down = lax.ppermute(send, "row", [(rows - d, rows - d - 1)])
        tail = tail + up + down
    tail = tail.reshape(days, pairs, 2, all_pairs)

    todo = []
    for k in range(pairs):
        for d in range(1, rows):
            todo.append((2 * d + (rows - 1) * k, k))
    for _, k in sorted(todo):
        if len(chunks[k].left) == 1 or k > 0 or len(chunks[k].left) < rows:
            if len(chunks[k].left) < rows:
                run(chunks[k])

    leg_all = jnp.concatenate(leg.slots(), axis=0)
    if share:
        leg.left, leg.right = swapped_left, swapped_right
        other_own = lax.dynamic_slice(legendre, (0, (1 - e) * half), (cycles, half))
        leg.left[0] = leg.right[0] = other_own
        leg_other = jnp.concatenate(leg.slots(), axis=0)
        leg_all = jnp.where(
            e == 0,
            jnp.concatenate([leg_all, leg_other], axis=1),
            jnp.concatenate([leg_other, leg_all], axis=1),
        )

    column = lax.broadcasted_iota(jnp.int32, (1, degree_cols), 1)
    day = lax.broadcasted_iota(jnp.int32, (days, 1), 0)

    def residual(block, pair):
        weights = lax.dynamic_slice(
            lag_weights, (0, pair * 2 * degree_cols), (3, 2 * degree_cols)
        )
        lg = lax.dynamic_slice(leg_all, (0, pair * degree_cols), (leg_all.shape[0], degree_cols))
        ends = lax.dynamic_index_in_dim(tail, pair, 1, False)
        edge = lax.dynamic_index_in_dim(boundary, pair, 0, False)
        out = []
        for w in range(2):
            s = lax.dot_general(
                block[:, w * days : (w + 1) * days],
                lg,
                (((0,), (0,)), ((), ())),
                preferred_element_type=jnp.float32,
            )
            padded = jnp.pad(ends[:, w], ((0, 0), (lead, 0)))
            s = jnp.where(column < edge, s, padded)
            a = weights[:, w * degree_cols : (w + 1) * degree_cols]
            before = [jnp.pad(s[: days - i], ((i, 0), (0, 0))) for i in (1, 2, 3)]
            r = s - a[0] * before[0] - a[1] * before[1] - a[2] * before[2]
            out.append(jnp.where(day >= 3, r, 0.0).astype(jnp.bfloat16))
        return jnp.concatenate(out, axis=1)

    full = [jnp.concatenate(line.slots(), axis=0) for line in chunks]
    parts = [residual(full[k], order[k]) for k in range(pairs)]

    is_early = jnp.asarray(early)[z]
    lhs = []
    for h in range(row_pairs):
        if late:
            there = jnp.concatenate([s[h] for s in early_rows.slots()], axis=0)
            r = residual(jnp.where(is_early, full[h], there), row_first + h)
        else:
            r = parts[h]
        held = [{owner[i]} for i in range(rows)]
        bit = cols // 2
        while bit:
            route = [(i * cols + s, i * cols + (s ^ bit)) for i in range(rows) for s in held[i]]
            got = lax.ppermute(r, ("row", "col"), route)
            mask = sum(
                jnp.where((z == i) & (c == (s ^ bit)), 1, 0) for i in range(rows) for s in held[i]
            )
            r = jnp.where(mask > 0, got, r)
            held = [h_ | {s ^ bit for s in h_} for h_ in held]
            bit //= 2
        lhs.append(r.T)
    lhs = jnp.concatenate(lhs, axis=0)
    lhs_next = jnp.pad(lhs[:, 1:], ((0, 0), (0, 1)))

    outs = None
    for k in range(pairs):
        place = order[k].reshape(1).astype(jnp.int32)
        outs = covariance(place, lhs, lhs_next, parts[k], outs, part_cols)
    return tuple(outs)


def solution(mesh):
    in_specs = (P("row", "col", "ens"), P("row", "col"), P(None, "col"), P("col"))
    out_specs = (P(("ens", "row"), "col"), P(("ens", "row"), "col"))
    return jax.shard_map(body, mesh=mesh, in_specs=in_specs, out_specs=out_specs, check_vma=False)
```

```python
import functools

import jax
import jax.numpy as jnp
from jax import lax
from jax.experimental import pallas as pl
from jax.experimental.pallas import tpu as pltpu
from jax.sharding import PartitionSpec as P


ODD, INNER, SOURCE, STEPS = 0, 1, 2, 3
F32 = jnp.float32
BF16 = jnp.bfloat16


def cov_kernel(tasks, sources, tiles, places, flags, *refs):
    groups = len(places)
    halves = sorted({m // groups for m in tasks})
    lhs = refs[: len(halves) * sources]
    cols = refs[len(halves) * sources :][:groups]
    outs = refs[-7:-5]
    held, chunks, buf, sems, out_sems = refs[-5:]
    days, chunk = chunks.shape[1:]
    tile = held.shape[1]
    base = halves[0] * tiles
    first = tasks[0]
    used = []
    for m in tasks:
        if m % groups not in used:
            used.append(m % groups)

    def col_copy(g):
        return pltpu.make_async_copy(cols[g], chunks.at[g], sems.at[held.shape[0] + g])

    def fetch(h):
        for i in range(sources):

            @pl.when(flags[SOURCE] == i)
            def _(i=i):
                for t in range(tiles):
                    n = h * tiles + t - base
                    pltpu.make_async_copy(
                        lhs[(h - halves[0]) * sources + i].at[pl.ds(t * tile, tile)],
                        held.at[n],
                        sems.at[n],
                    ).start()

    fetch(halves[0])
    for g in used:
        col_copy(g).start()
    for h in halves[1:]:
        fetch(h)

    def out_copy(s, which):
        m = first + s // tiles
        begin = pl.multiple_of((m // groups * tiles + s % tiles) * tile, 16)
        place = flags[places[0] + (places[-1] - places[0]) * (m % groups)]
        column = pl.multiple_of(place * chunk, 128)
        return pltpu.make_async_copy(
            buf.at[s % 2, which],
            outs[which].at[pl.ds(begin, tile), pl.ds(column, chunk)],
            out_sems.at[s % 2, which],
        )

    steps = len(tasks) * tiles

    @pl.loop(0, steps)
    def _(s):
        m = first + s // tiles
        g = m % groups
        n = m // groups * tiles + s % tiles - base

        @pl.when((m == first) | (g == 0))
        def _():
            pltpu.make_async_copy(held.at[n], held.at[n], sems.at[n]).wait()

        @pl.when((s % tiles == 0) & (m - first < len(used)))
        def _():
            which = chunks.at[g]
            pltpu.make_async_copy(which, which, sems.at[held.shape[0] + g]).wait()

        @pl.when(s >= 2)
        def _():
            for which in range(2):
                out_copy(s - 2, which).wait()

        now = held[n]
        later = pltpu.roll(now.astype(F32), days - 1, 1).astype(BF16)
        for which, lines in enumerate((now, later)):
            buf[s % 2, which] = (
                jnp.dot(lines, chunks[g], preferred_element_type=F32)
                * (1.0 / (days - 3 - which))
            ).astype(BF16)
        for which in range(2):
            out_copy(s, which).start()

    for s in range(steps - 2, steps):
        for which in range(2):
            out_copy(s, which).wait()


def covariance(flags, places, tasks, lhs, cols, outs, shape):
    rows, days = lhs[0][0].shape
    chunk = cols[0].shape[1]
    groups = len(cols)
    sources = len(lhs[0])
    tiles = 4
    tile = rows // tiles
    halves = sorted({m // groups for m in tasks})
    anywhere = pl.BlockSpec(memory_space=pltpu.HBM)
    operands = [flags] + [x for h in halves for x in lhs[h]] + list(cols)
    aliases = {}
    if outs is not None:
        aliases = {len(operands): 0, 1 + len(operands): 1}
        operands += list(outs)
    shape = jax.ShapeDtypeStruct(shape, BF16)
    return pl.pallas_call(
        functools.partial(cov_kernel, tasks, sources, tiles, places),
        in_specs=[pl.BlockSpec(memory_space=pltpu.SMEM)] + [anywhere] * (len(operands) - 1),
        out_specs=[anywhere] * 2,
        scratch_shapes=[
            pltpu.VMEM((len(halves) * tiles, tile, days), BF16),
            pltpu.VMEM((groups, days, chunk), BF16),
            pltpu.VMEM((2, 2, tile, chunk), BF16),
            pltpu.SemaphoreType.DMA((len(halves) * tiles + groups,)),
            pltpu.SemaphoreType.DMA((2, 2)),
        ],
        out_shape=[shape, shape],
        input_output_aliases=aliases,
        compiler_params=pltpu.CompilerParams(vmem_limit_bytes=56 * 1024 * 1024),
        cost_estimate=pl.CostEstimate(
            flops=4 * len(tasks) * rows * days * chunk,
            bytes_accessed=4 * len(tasks) * rows * chunk,
            transcendentals=0,
        ),
    )(*operands)


def prepare_kernel(pairs, flags, spectra, even_out, odd_out):
    days = spectra.shape[2]
    half = pairs // 2
    for p in range(pairs):
        position = lax.rem(p // 2 + flags[ODD], half)
        for w in range(2):
            begin = pl.multiple_of((2 * position + w) * days, 128)
            (odd_out if p % 2 else even_out)[:, pl.ds(begin, days)] = spectra[:, 4 * p + w, :]


def prepare(flags, fourier, pairs):
    cycles, _, days = fourier.shape
    vmem = pl.BlockSpec(memory_space=pltpu.VMEM)
    block = jax.ShapeDtypeStruct((cycles, pairs * days), BF16)
    return pl.pallas_call(
        functools.partial(prepare_kernel, pairs),
        in_specs=[pl.BlockSpec(memory_space=pltpu.SMEM), vmem],
        out_specs=[vmem] * 2,
        out_shape=[block, block],
        compiler_params=pltpu.CompilerParams(vmem_limit_bytes=56 * 1024 * 1024),
        cost_estimate=pl.CostEstimate(flops=0, bytes_accessed=4 * fourier.size, transcendentals=0),
        name="prepare",
    )(flags, fourier)


def edge_kernel(pairs, ends, spectra, legendre, sums, tiles, sems):
    cycles, _, _ = spectra.shape
    degree_cols = legendre.shape[1] // pairs
    lanes = tiles.shape[2]
    begins = [(p + 1) * degree_cols - ends for p in range(pairs)]
    copies = []
    for p, begin in enumerate(begins):
        copies.append(
            pltpu.make_async_copy(
                legendre.at[:, pl.ds(begin // lanes * lanes, lanes)], tiles.at[p], sems.at[p]
            )
        )
        copies[-1].start()
    lane = lax.broadcasted_iota(jnp.int32, (cycles, lanes), 1) // ends
    total = jnp.zeros(sums.shape, F32)
    for p in range(pairs):
        copies[p].wait()
        last = tiles[p].astype(F32)
        for w in range(2):
            shift = ((2 * p + w) * ends - begins[p]) % lanes
            moved = pltpu.roll(last, shift, 1) if shift else last
            total = total + lax.dot_general(
                spectra[:, 4 * p + 2 + w, :],
                jnp.where(lane == 2 * p + w, moved, 0.0).astype(BF16),
                (((0,), (0,)), ((), ())),
                preferred_element_type=F32,
            )
    sums[...] = total


def edge_sums(fourier, legendre, pairs, ends):
    cycles, _, days = fourier.shape
    vmem = pl.BlockSpec(memory_space=pltpu.VMEM)
    lanes = 2 * pairs * ends
    return pl.pallas_call(
        functools.partial(edge_kernel, pairs, ends),
        in_specs=[vmem, pl.BlockSpec(memory_space=pltpu.HBM)],
        out_specs=vmem,
        out_shape=jax.ShapeDtypeStruct((days, lanes), F32),
        scratch_shapes=[
            pltpu.VMEM((pairs, cycles, lanes), BF16),
            pltpu.SemaphoreType.DMA((pairs,)),
        ],
        compiler_params=pltpu.CompilerParams(vmem_limit_bytes=56 * 1024 * 1024),
        cost_estimate=pl.CostEstimate(
            flops=8 * pairs * cycles * days * ends, bytes_accessed=2 * fourier.size, transcendentals=0
        ),
        name="edge_sums",
    )(fourier, legendre)


def analyse_kernel(plan, flags, pair_order, weights, *refs):
    tails = refs[: plan.tails]
    refs = refs[plan.tails :]
    operands = refs[: plan.operands]
    outs = refs[-plan.outs - 6 : -6]
    fbuf, lbuf, rbuf, tbuf, sems, out_sems = refs[-6:]
    pair = flags[STEPS + 3 * plan.step]
    degree_cols = plan.degree_cols
    edge = degree_cols - 1 - pair_order[pair]

    def copies(entry, number):
        into = (fbuf if entry.buffer == 0 else lbuf).at[entry.slot]
        source = operands[entry.operand]
        if entry.index is not None:
            source = source.at[entry.index]
        else:
            begin = entry.offset
            if entry.scaled is not None:
                begin = pl.multiple_of(begin + flags[entry.scaled] * 2 * degree_cols, 128)
            source = source.at[:, pl.ds(begin, into.shape[1])]
        return pltpu.make_async_copy(source, into, sems.at[number])

    slots = {}
    for entry in plan.entries:
        number = slots.setdefault((entry.buffer, entry.slot), len(slots))
        hit = None
        for flag, value in entry.when:
            same = flags[flag] == value
            hit = same if hit is None else hit & same
        if hit is None:
            copies(entry, number).start()
        else:
            pl.when(hit)(lambda entry=entry, number=number: copies(entry, number).start())

    def arrived(buffer, slot):
        whole = (fbuf if buffer == 0 else lbuf).at[slot]
        pltpu.make_async_copy(whole, whole, sems.at[slots[buffer, slot]]).wait()

    days = fbuf.shape[2] // 2
    blocks = fbuf.shape[0]
    wide = lbuf.shape[2]
    shift = wide - degree_cols
    mine = weights[:, pl.ds(pl.multiple_of(pair * 2 * degree_cols, 128), 2 * degree_cols)]
    tail = tails[0][...]
    for more in tails[1:]:
        tail = tail + more[...]
    tile_lane = lax.broadcasted_iota(jnp.int32, (days, 128), 1)

    def ends(w, s):
        begin = (w + 1) * degree_cols - plan.ends
        first = begin // 128 * 128
        turn = lax.rem(begin - first - (2 * pair + w) * plan.ends + tail.shape[1], tail.shape[1])
        column = first + tile_lane - w * degree_cols
        return jnp.where(column < edge, s, pltpu.roll(tail, turn, 1))

    out_copies = []

    def finish(s, begin):
        end = begin + s.shape[1]
        day = lax.broadcasted_iota(jnp.int32, s.shape, 0)
        a = mine[:, begin:end]
        r = s
        for i in range(3):
            r = r - a[i : i + 1] * pltpu.roll(s, i + 1, 0)
        r = jnp.where(day >= 3, r, 0.0)
        rbuf[:, begin:end] = r.astype(BF16)
        into = pl.ds(plan.column + begin, end - begin)
        here = pl.ds(begin, end - begin)
        out_copies.append(
            pltpu.make_async_copy(
                rbuf.at[:, here], outs[0].at[:, into], out_sems.at[len(out_copies)]
            )
        )
        out_copies[-1].start()
        if plan.outs == 2:
            tbuf[begin:end, :] = r.T.astype(BF16)
            out_copies.append(
                pltpu.make_async_copy(
                    tbuf.at[here], outs[1].at[here], out_sems.at[len(out_copies)]
                )
            )
            out_copies[-1].start()

    for w in range(2):
        s = jnp.zeros((days, wide), F32)
        for b in range(blocks):
            if w == 0:
                arrived(0, b)
                arrived(1, b)
            lg = lbuf[b]
            if plan.odd != w:
                turn = shift if w else wide - shift
                lg = pltpu.roll(lg.astype(F32), turn, 1).astype(BF16)
            s = s + lax.dot_general(
                fbuf[b, :, w * days : (w + 1) * days],
                lg,
                (((0,), (0,)), ((), ())),
                preferred_element_type=F32,
            )
        if w == 0:
            finish(s[:, : wide - 128], 0)
            middle = ends(0, s[:, wide - 128 :])
        else:
            s = jnp.concatenate(
                [jnp.where(tile_lane < 128 - shift, middle, s[:, :128]), s[:, 128 : wide - 128], ends(1, s[:, wide - 128 :])], axis=1
            )
            finish(s, wide - 128)
    for copy in out_copies:
        copy.wait()


class Entry:
    def __init__(self, buffer, slot, operand, when=(), offset=0, scaled=None, index=None):
        self.buffer, self.slot, self.operand, self.when = buffer, slot, operand, when
        self.offset, self.scaled, self.index = offset, scaled, index


class Plan:
    def __init__(self, entries, operands, tails, ends, step, degree_cols, outs, column, odd):
        self.entries, self.operands, self.ends = entries, operands, ends
        self.tails, self.step, self.degree_cols = tails, step, degree_cols
        self.outs, self.column, self.odd = outs, column, odd


def analyse(
    entries, k, group, odd, transposed, held, flags, pair_order, weights, tails, ends, operands, blocks
):
    days = tails[0].shape[0]
    degree_cols = weights.shape[1] // pair_order.shape[0] // 2
    wide = degree_cols + degree_cols % 128
    cycles = operands[0].shape[-2]
    column = (k % group) * 2 * degree_cols
    plan = Plan(
        entries, len(operands), len(tails), ends, k, degree_cols, 1 + transposed, column, odd
    )
    shapes = [jax.ShapeDtypeStruct((days, group * 2 * degree_cols), BF16)]
    if transposed:
        shapes.append(jax.ShapeDtypeStruct((2 * degree_cols, days), BF16))
    vmem = pl.BlockSpec(memory_space=pltpu.VMEM)
    hbm = pl.BlockSpec(memory_space=pltpu.HBM)
    given = [flags, pair_order, weights, *tails, *operands]
    aliases = {}
    if held is not None:
        aliases = {len(given): 0}
        given.append(held)
    return pl.pallas_call(
        functools.partial(analyse_kernel, plan),
        in_specs=[pl.BlockSpec(memory_space=pltpu.SMEM)] * 2
        + [vmem] * (1 + len(tails))
        + [hbm] * (len(given) - 3 - len(tails)),
        out_specs=[hbm] * len(shapes),
        out_shape=shapes,
        input_output_aliases=aliases,
        scratch_shapes=[
            pltpu.VMEM((blocks, cycles, 2 * days), BF16),
            pltpu.VMEM((blocks, cycles, wide), BF16),
            pltpu.VMEM((days, 2 * degree_cols), BF16),
            pltpu.VMEM((2 * degree_cols if transposed else 16, days), BF16),
            pltpu.SemaphoreType.DMA((2 * blocks,)),
            pltpu.SemaphoreType.DMA((4,)),
        ],
        compiler_params=pltpu.CompilerParams(vmem_limit_bytes=56 * 1024 * 1024),
        cost_estimate=pl.CostEstimate(
            flops=4 * days * degree_cols * cycles * blocks,
            bytes_accessed=8 * blocks * cycles * days,
            transcendentals=0,
        ),
    )(*given)


def body(fourier, legendre, lag_weights, pair_order):
    cycles, _, days = fourier.shape
    pairs = pair_order.shape[0]
    degree_cols = legendre.shape[1] // pairs
    part_cols = lag_weights.shape[1]
    rows, cols, members = (lax.axis_size(a) for a in ("row", "col", "ens"))
    z, c, e = (lax.axis_index(a) for a in ("row", "col", "ens"))
    all_pairs = pairs * cols
    lead = degree_cols - all_pairs
    row_pairs = all_pairs // 2 // rows
    owner = [r * row_pairs // pairs for r in range(rows)]
    local = [r * row_pairs % pairs for r in range(rows)]
    paired = rows == 4 and members == 2 and pairs == 4 and row_pairs == 2

    spectra = fourier.reshape(cycles, pairs, 2, 2, days)
    last = legendre.reshape(cycles, pairs, degree_cols)[:, :, lead:]

    def tail_part():
        part = jnp.einsum("cpwd,cpj->pwdj", spectra[:, :, 1], last, preferred_element_type=F32)
        return part.transpose(2, 0, 1, 3).reshape(days, pairs * 2 * all_pairs)

    def tail_whole(tail):
        lanes = -tail.shape[1] % 128
        return jnp.pad(tail, ((0, 0), (0, lanes))) if lanes else tail


    where = {}

    def table(steps):
        made = [
            [
                [
                    [owner_odd(cc), inner_row(rr), where[rr][cc]]
                    + [v for k in range(pairs) for v in steps(rr, cc, ee, k)]
                    for ee in range(members)
                ]
                for cc in range(cols)
            ]
            for rr in range(rows)
        ]
        return jnp.asarray(made, jnp.int32)[z, c, e]

    def owner_odd(cc):
        return cc % 2

    def inner_row(rr):
        return int(0 < rr < rows - 1)

    def spread_plan():
        found = [{owner[i]: 0} for i in range(rows)]
        hops, count, bit = [], 1, cols // 2
        while bit:
            for n in range(count):
                route = []
                for i in range(rows):
                    for s in [s for s, m in found[i].items() if m == n]:
                        route.append((i * cols + s, i * cols + (s ^ bit)))
                        found[i][s ^ bit] = count + n
                hops.append((f"{bit}_{n}", n, route))
            count *= 2
            bit //= 2
        return found, hops

    where, hops = spread_plan()
    results = []
    if paired:
        half = pairs // 2 * degree_cols
        swap_ends = [(0, 1), (1, 0), (2, 3), (3, 2)]
        swap_middle = [(1, 2), (2, 1)]
        outward = [(1, 0), (2, 3)]
        other_member = [(0, 1), (1, 0)]

        def steps(rr, cc, ee, k):
            pair = ((k + 2) % 4 * inner_row(rr) + k * (1 - inner_row(rr)) + 2 * (cc % 2)) % 4
            return pair, pair // 2, int(pair // 2 == ee)

        flags = table(steps)
        mine = lax.dynamic_slice(legendre, (0, e * half), (cycles, half))
        leg_a = lax.ppermute(mine, "row", swap_ends)
        ordered = prepare(flags, fourier, pairs)
        part = edge_sums(fourier, legendre, pairs, all_pairs)
        four_a = [lax.ppermute(ordered[i], "row", swap_ends) for i in range(2)]
        leg_b = [lax.ppermute(x, "row", swap_middle) for x in (mine, leg_a)]
        leg_a_other = lax.ppermute(leg_a, "ens", other_member)
        leg_c = [lax.ppermute(x, "row", outward) for x in leg_b]
        both_members = lambda rs: [(2 * r + m, 2 * r + 1 - m) for r in rs for m in (0, 1)]
        leg_b_other = [lax.ppermute(x, ("row", "ens"), both_members((1, 2))) for x in leg_b]
        leg_c_other = [lax.ppermute(x, ("row", "ens"), both_members((0, 3))) for x in leg_c]

        got = lax.ppermute(part, "row", [(0, 1), (3, 2)])
        near = lax.ppermute(part + got, "row", swap_middle)
        far = lax.ppermute(part + near, "row", outward)
        tails = [part, got, near, far]

        four_b, four_c = [None] * 4, [None] * 4
        for j in (0, 2, 1, 3):
            there = slice((j // 2) * 2 * days, (j // 2 + 1) * 2 * days)
            both = jnp.concatenate([ordered[j % 2][:, there], four_a[j % 2][:, there]], axis=1)
            four_b[j] = lax.ppermute(both, "row", swap_middle)
        for j in range(4):
            four_c[j] = lax.ppermute(four_b[j], "row", outward)

        group = 2

        def step(k, held):
            j_in = (k + 2) % 4
            odd = k % 2
            same = STEPS + 3 * k + 2
            lanes = 2 * days
            offset = odd * (degree_cols - degree_cols % 128)
            operands = [
                ordered[k % 2], four_a[k % 2], four_b[j_in], four_c[k],
                legendre, leg_a, leg_a_other,
                *leg_b, *leg_c, *leg_b_other, *leg_c_other,
            ]
            entries = [
                Entry(0, 0, 0, ((INNER, 0),), (k // 2) * lanes),
                Entry(0, 0, 0, ((INNER, 1),), (j_in // 2) * lanes),
                Entry(1, 0, 4, (), offset, STEPS + 3 * k + 1),
                Entry(0, 1, 1, ((INNER, 0),), (k // 2) * lanes),
                Entry(0, 1, 1, ((INNER, 1),), (j_in // 2) * lanes),
                Entry(1, 1, 5, ((same, 1),), offset),
                Entry(1, 1, 6, ((same, 0),), offset),
            ]
            for b in range(2):
                entries += [
                    Entry(0, 2 + b, 2, ((INNER, 1),), b * lanes),
                    Entry(0, 2 + b, 3, ((INNER, 0),), b * lanes),
                ]
                for n, (own, inner) in enumerate(((1, 1), (1, 0), (0, 1), (0, 0))):
                    entries.append(
                        Entry(1, 2 + b, 7 + 2 * n + b, ((same, own), (INNER, inner)), offset)
                    )
            return analyse(
                entries, k, group, odd, k < row_pairs, held, flags, pair_order, lag_weights,
                tails, all_pairs, operands, 4,
            )
    else:
        zeroth = spectra[:, :, 0].transpose(1, 0, 2, 3).reshape(pairs, cycles, 2 * days)
        four = lax.all_gather(zeroth, "row", axis=0)
        leg = lax.all_gather(legendre, "row", axis=0)
        tail = tail_whole(lax.psum(tail_part(), "row"))
        flags = table(lambda rr, cc, ee, k: ((local[rr] + k) % pairs, 0, 0))

        group = 1

        def step(k, held):
            pair = flags[STEPS + 3 * k]
            block = lax.dynamic_index_in_dim(four, pair, 1, False)
            lg = lax.dynamic_slice(
                leg, (0, 0, pair * degree_cols), (rows, cycles, degree_cols)
            )
            lg = jnp.pad(lg, ((0, 0), (0, 0), (0, degree_cols % 128)))
            entries = []
            for b in range(rows):
                entries += [Entry(0, b, 0, index=b), Entry(1, b, 1, index=b)]
            return analyse(
                entries, k, group, 0, k < row_pairs, held, flags, pair_order, lag_weights, [tail],
                all_pairs, [block, lg], rows,
            )

    lhs = []
    for k in range(pairs):
        outs = step(k, results[-1] if k % group else None)
        if k % group:
            results[-1] = outs[0]
        else:
            results.append(outs[0])
        if k < row_pairs:
            arrays = [outs[1]]
            for name, n, route in hops:
                arrays.append(lax.ppermute(arrays[n], ("row", "col"), route))
            lhs.append(arrays)

    shape = (row_pairs * 2 * degree_cols, part_cols)
    outs = None
    places = [STEPS + 3 * g * group + (1 if group == 2 else 0) for g in range(len(results))]
    count = row_pairs * len(results)
    for name, tasks in (("cov_a", [0]), ("cov_b", list(range(1, count)))):
        if tasks:
            cols_of = results if name == "cov_b" else results[:1]
            outs = covariance(flags, places[: len(cols_of)], tasks, lhs, cols_of, outs, shape)
    return tuple(outs)


def solution(mesh):
    in_specs = (P("row", "col", "ens"), P("row", "col"), P(None, "col"), P("col"))
    out_specs = (P(("ens", "row"), "col"), P(("ens", "row"), "col"))
    return jax.shard_map(body, mesh=mesh, in_specs=in_specs, out_specs=out_specs, check_vma=False)
```
